512 devices in a mesh: sweep: 16 (over z, core), lat: 32 (over y, x).
Axes of the slice: x: 4, y: 8, z: 8, core: 2. Of those that a mesh axis runs over, the one named last changes fastest.
Arguments:
- traveltime: float32 [2, 128, 512, 384], P(None, 'sweep', 'lat'), may hold values from 0 to 4
- residual: float32 [2, 128, 512, 384], P(None, 'sweep', 'lat'), may hold values from -6 to 6
- slowness: float32 [128, 512, 384], P('sweep', 'lat'), may hold values from 0.3 to 0.6
- attenuation: float32 [128, 512, 384], P('sweep', 'lat'), may hold values from 0.005 to 0.05
- topography: int32 [512, 384], P('lat'), may hold values from 0 to 127, as said below
Outputs:
- adjoint: float32 [2, 128, 512, 384], P(None, 'sweep', 'lat')
- gradient: float32 [128, 512, 384], P('sweep', 'lat')
The draws below stay inside these ranges and needn't reach their ends.
Inputs may be any that keep to these rules, and one draw needn't show every extreme that they name: Apart from two corner columns, topography is a level shared by each aligned strip of 16 columns along the first lateral dimension plus a small rough offset per column, so that whole blocks of planes lie above it; the first column of the grid has topography 128 - 1 and the last column 0.
All inputs are finite; a program needn't handle non-finite values.
Results may differ from the reference program's by a relative error of at most 0.0003.
Values sent between devices are 32-bit elements; how exact they have to be, the bound alone decides.
No kernel may reach another device: no remote copies, remote signals or barrier semaphores. Data moves between devices by JAX's collectives and lax.ppermute only.
A program may use at most 64 MiB of HBM per device.

```python
import math
import jax
import jax.numpy as jnp
from jax import lax

SOURCES = 2
COLS_DEV = 16
NY = 384
NX = 512
NZ = 128


def draw_traveltime(key, part):
    key_parity = jax.random.fold_in(key, 21)
    key_value = jax.random.fold_in(key, 22)
    shape = (SOURCES, NZ, NX, NY)
    parity = jax.random.randint(key_parity, (SOURCES, 1, 1, 1), 0, 2)
    row_ids = lax.broadcasted_iota(jnp.int32, shape, 3)
    raised = (row_ids + parity) % 2 == 0
    uniform_part = jax.random.uniform(key_value, shape, jnp.float32)
    high_values = 3.4 + 0.6 * uniform_part
    low_values = 0.6 * uniform_part
    field = jnp.where(raised, high_values, low_values)
    return field.astype(jnp.float32)


def draw_topography(key, part):
    key_base = jax.random.fold_in(key, 11)
    key_bump = jax.random.fold_in(key, 12)
    strips = NX // COLS_DEV
    levels = jax.random.randint(key_base, (strips,), 0, 3 * NZ // 4)
    bumps = jax.random.randint(key_bump, (NX, NY), 0, NZ // 8 + 1)
    field = jnp.repeat(levels, COLS_DEV)[:, None] + bumps
    row_ids = lax.broadcasted_iota(jnp.int32, (NX, NY), 0)
    col_ids = lax.broadcasted_iota(jnp.int32, (NX, NY), 1)
    field = jnp.where((row_ids == 0) & (col_ids == 0), NZ - 1, field)
    field = jnp.where((row_ids == NX - 1) & (col_ids == NY - 1), 0, field)
    return field.astype(jnp.int32)


def block_levels(stream_key, extent, shards, smallest, largest):
    gain, own = 1.0, jax.random.fold_in(stream_key, 6)
    for dim, blocks in shards:
        heights = jnp.exp(jax.random.uniform(jax.random.fold_in(own, dim), (blocks,), jnp.float32, smallest / len(shards), largest / len(shards)))
        gain = gain * jnp.repeat(heights, extent[dim] // blocks).reshape([-1 if axis == dim else 1 for axis in range(len(extent))])
    return gain


def scatter_about(key, shape, width, bound, shards=(), held_as=jnp.bfloat16):
    gain = block_levels(key, shape, shards, -0.22, 0.18) if shards else 1.0
    values = jax.random.normal(key, shape, jnp.float32) * width * gain
    return jnp.minimum(jnp.maximum(values, -bound), bound).astype(held_as)


def setup_inputs(seed: int = 0) -> dict:
    seeds = jax.random.split(jax.random.key(seed), 6)
    traveltime = draw_traveltime(jax.random.fold_in(seeds[5], 71), 0)
    residual = scatter_about(seeds[1], (SOURCES, NZ, NX, NY), 1.0, 6.0, ((1, 16), (2, 32)), jnp.float32)
    slowness = jnp.clip(jnp.exp(math.log(0.6) - 0.6931472 * jax.random.uniform(seeds[2], (NZ, NX, NY), jnp.float32) ** block_levels(seeds[2], (NZ, NX, NY), ((0, 16), (1, 32)), -0.2, 0.2)), 0.3, 0.6)
    attenuation = jnp.clip(jnp.exp(math.log(0.05) - 2.3025851 * jax.random.uniform(seeds[3], (NZ, NX, NY), jnp.float32) ** block_levels(seeds[3], (NZ, NX, NY), ((0, 16), (1, 32)), -0.2, 0.2)), 0.005, 0.05)
    topography = draw_topography(jax.random.fold_in(seeds[5], 71), 0)
    return dict(traveltime=traveltime, residual=residual, slowness=slowness, attenuation=attenuation, topography=topography)


def shift_low(field, along):
    count = field.shape[along]
    padding = jnp.zeros_like(lax.slice_in_dim(field, 0, 1, axis=along))
    return jnp.concatenate([padding, lax.slice_in_dim(field, 0, count - 1, axis=along)], axis=along)


def shift_high(field, along):
    count = field.shape[along]
    padding = jnp.zeros_like(lax.slice_in_dim(field, 0, 1, axis=along))
    return jnp.concatenate([lax.slice_in_dim(field, 1, count, axis=along), padding], axis=along)


def upwind_weights(tau_wide):
    last = tau_wide.ndim - 1
    center = tau_wide[..., 1:-1, :]
    west = jax.nn.softplus(center - tau_wide[..., :-2, :])
    east = jax.nn.softplus(center - tau_wide[..., 2:, :])
    north = jax.nn.softplus(center - shift_low(center, last))
    south = jax.nn.softplus(center - shift_high(center, last))
    return west, east, north, south


def reference(traveltime, residual, slowness, attenuation, topography):
    sources = traveltime.shape[0]

    def advance(previous, inputs):
        tau_plane, source_plane, slow_plane, atten_plane, plane_index = inputs
        tau_wide = jnp.pad(tau_plane, ((0, 0), (1, 1), (0, 0)))
        west, east, north, south = upwind_weights(tau_wide)
        active = (plane_index >= topography).astype(jnp.float32)
        denominator = slow_plane + west + east + north + south + atten_plane
        scale = active / denominator
        current = scale * (source_plane + slow_plane * previous + west * shift_low(previous, 1)
                           + east * shift_high(previous, 1) + north * shift_low(previous, 2)
                           + south * shift_high(previous, 2))
        return current, current

    inputs = (jnp.moveaxis(traveltime, 1, 0), jnp.moveaxis(residual, 1, 0), slowness, attenuation,
              jnp.arange(slowness.shape[0], dtype=jnp.int32))
    start = jnp.zeros((sources, slowness.shape[1], slowness.shape[2]), jnp.float32)
    _, planes_out = lax.scan(advance, start, inputs)
    adjoint = jnp.moveaxis(planes_out, 0, 1)
    gradient = slowness * jnp.sum(adjoint, axis=0)
    return adjoint, gradient
```

```python
import functools
import jax
import jax.numpy as jnp
from jax import lax
from jax.experimental import pallas as pl
from jax.experimental.pallas import tpu as pltpu
from jax.sharding import PartitionSpec as P

F32 = jnp.float32
VM = pltpu.VMEM
HALF = 8
DEEP = 16
COLS = 16
ROWS = 8 * DEEP + 8
AXES = ("sweep", "lat")


def whole(count):
    return [pl.BlockSpec(memory_space=VM)] * count


def place():
    s = lax.axis_index("sweep")
    return s // 2, s % 2


def split_kernel(tau, res, slow, att, near_ref, away_ref, sems):
    _, core = place()
    copies = []
    for k, (out, side) in enumerate(((away_ref, 1 - core), (near_ref, core))):
        for a, src in enumerate((tau.at[side], res.at[side], slow, att)):
            copies.append(pltpu.make_async_copy(src, out.at[a], sems.at[4 * k + a]))
    for copy in copies:
        copy.start()
    for copy in copies:
        copy.wait()


def pack_kernel(topo_ref, own_ref, got_ref, mid_ref, right_ref, left_ref):
    _, core = place()
    near, far = core * HALF, (1 - core) * HALF
    mid_ref[:, pl.ds(near, HALF)] = own_ref[...]
    mid_ref[:, pl.ds(far, HALF)] = got_ref[...]
    row = lax.broadcasted_iota(jnp.int32, (COLS, topo_ref.shape[1]), 0)
    for a in range(4):
        base = a * ROWS
        right_ref[base : base + COLS] = mid_ref[a, 0]
        left_ref[base : base + COLS] = mid_ref[a, 0]
        for j in range(1, 8):
            at = base + COLS * j
            near_plane, far_plane = mid_ref[a, j], mid_ref[a, DEEP - j]
            right_ref[at : at + COLS] = jnp.where(row >= j, near_plane, pltpu.roll(far_plane, j, 0))
            left_ref[at : at + COLS] = jnp.where(row < COLS - j, near_plane, pltpu.roll(far_plane, COLS - j, 0))
        at = base + COLS * 8
        right_ref[at : at + 8] = mid_ref[a, 8, 8:16]
        left_ref[at : at + 8] = mid_ref[a, 8, 0:8]
    topo = topo_ref[...].astype(F32)
    right_ref[4 * ROWS : 4 * ROWS + COLS] = topo
    left_ref[4 * ROWS : 4 * ROWS + COLS] = topo


def band(j):
    halo = 15 - j
    trim = 0 if halo > 8 else 8 if halo > 0 else 16
    return trim, 3 * COLS - trim


def coef_kernel(mid_ref, west_ref, east_ref, topo_ref, src_o, mid_o, west_o, east_o, north_o, south_o):
    depth, lat, lats = place()[0] * DEEP, lax.axis_index("lat"), lax.axis_size("lat")
    rows = topo_ref.shape[1]
    wide = (3 * COLS, rows)
    col = lax.broadcasted_iota(jnp.int32, wide, 0)
    cross = lax.broadcasted_iota(jnp.int32, wide, 1)
    first, last = cross == 0, cross == rows - 1
    inside = ((col >= COLS) | (lat > 0)) & ((col < 2 * COLS) | (lat < lats - 1))
    top = 4 * ROWS
    topo = jnp.concatenate([west_ref[top : top + COLS], topo_ref[...].astype(F32), east_ref[top : top + COLS]], axis=0)
    topo = jnp.where(inside, topo, 1e6)

    def window(a, j):
        base = a * ROWS
        if j <= 7:
            at = base + COLS * j
            west, east = west_ref[at : at + COLS], east_ref[at : at + COLS]
        elif j == 8:
            at = base + COLS * 8
            west, east = west_ref[at : at + 8], east_ref[at : at + 8]
            west, east = jnp.concatenate([west, west], axis=0), jnp.concatenate([east, east], axis=0)
        else:
            at = base + COLS * (DEEP - j)
            west = pltpu.roll(west_ref[at : at + COLS], j, 0)
            east = pltpu.roll(east_ref[at : at + COLS], DEEP - j, 0)
        return jnp.concatenate([west, mid_ref[a, j], east], axis=0)

    for j in range(DEEP):
        lo, hi = (0, 3 * COLS) if j < HALF else (8, 3 * COLS - 8)
        count = hi - lo
        tau = window(0, j)[lo:hi]
        slow = window(2, j)[lo:hi]
        active = (topo[lo:hi] <= (depth + j).astype(F32)).astype(F32)
        step_x = tau - pltpu.roll(tau, 1, 0)
        before = jnp.where(first[lo:hi], 0.0, pltpu.roll(tau, 1, 1))
        step_y = tau - before
        flat_x = jnp.log(1.0 + jnp.exp(-jnp.abs(step_x)))
        flat_y = jnp.log(1.0 + jnp.exp(-jnp.abs(step_y)))
        edge = tau[:, rows - 128 :]
        edge = jnp.maximum(edge, 0.0) + jnp.log(1.0 + jnp.exp(-jnp.abs(edge)))
        west = jnp.maximum(step_x, 0.0) + flat_x
        east = pltpu.roll(jnp.maximum(-step_x, 0.0) + flat_x, count - 1, 0)
        north = jnp.maximum(step_y, 0.0) + flat_y
        south = pltpu.roll(jnp.maximum(-step_y, 0.0) + flat_y, rows - 1, 1)
        edge = jnp.where(last[lo:hi, rows - 128 :], edge, south[:, rows - 128 :])
        south = jnp.concatenate([south[:, : rows - 128], edge], axis=1)
        scale = active / (slow + west + east + north + south + window(3, j)[lo:hi])
        src_o[j, lo:hi] = scale * window(1, j)[lo:hi]
        mid_o[j, lo:hi] = scale * slow
        west_o[j, lo:hi] = scale * west
        east_o[j, lo:hi] = scale * east
        north_o[j, lo:hi] = jnp.where(first[lo:hi], 0.0, scale * north)
        south_o[j, lo:hi] = jnp.where(last[lo:hi], 0.0, scale * south)


def sweep_kernel(turn, *refs):
    src, mid, west, east, north, south = refs[:6]
    keep_ref, give_ref, end_ref, buf_ref, sems = refs[-5:]
    stage, core = place()

    @pl.when(stage == turn)
    def _():
        rows = src.shape[2]
        if turn:
            level = jnp.concatenate([r[...] for r in refs[6:9]], axis=0)
        at = 0
        for j in range(DEEP):
            lo, hi = band(j)
            if turn == 0 and j == 0:
                level = src[j, lo:hi]
            else:
                count = level.shape[0]
                down, up = pltpu.roll(level, 1, 0), pltpu.roll(level, count - 1, 0)
                before, after = pltpu.roll(level, 1, 1), pltpu.roll(level, rows - 1, 1)
                cut = lo - at
                if cut:
                    level, down, up, before, after = (v[cut : count - cut] for v in (level, down, up, before, after))
                level = (
                    src[j, lo:hi]
                    + mid[j, lo:hi] * level
                    + west[j, lo:hi] * down
                    + east[j, lo:hi] * up
                    + north[j, lo:hi] * before
                    + south[j, lo:hi] * after
                )
            at = lo
            buf_ref[j] = level[COLS - lo : 2 * COLS - lo]
        end_ref[...] = level[COLS - at : 2 * COLS - at]
        kept = pltpu.make_async_copy(buf_ref.at[pl.ds(core * HALF, HALF)], keep_ref, sems.at[0])
        gave = pltpu.make_async_copy(buf_ref.at[pl.ds((1 - core) * HALF, HALF)], give_ref, sems.at[1])
        kept.start()
        gave.start()
        kept.wait()
        gave.wait()


def finish_kernel(kept_ref, got_ref, slow_ref, adjoint_ref, gradient_ref):
    _, core = place()
    own, got = kept_ref[...], got_ref[...]
    adjoint_ref[core] = own
    adjoint_ref[1 - core] = got
    gradient_ref[...] = slow_ref[...] * (own + got)


def shards(traveltime, residual, slowness, attenuation, topography):
    columns, crosses = topography.shape
    sweeps, lats = lax.axis_size("sweep"), lax.axis_size("lat")
    stages = sweeps // 2
    hbm = pl.BlockSpec(memory_space=pltpu.HBM)
    block = (HALF, columns, crosses)

    def shape(*dims):
        return jax.ShapeDtypeStruct(dims, F32)

    def call(kernel, outs, ins, vmem=4 << 20, in_specs=None, out_specs=None, **kw):
        return pl.pallas_call(
            kernel,
            out_shape=outs,
            in_specs=in_specs or whole(len(ins)),
            out_specs=out_specs or whole(len(outs)),
            compiler_params=pltpu.CompilerParams(vmem_limit_bytes=vmem),
            **kw,
        )(*ins)

    swap = [(i, i ^ 1) for i in range(sweeps)]
    near, away = call(
        split_kernel,
        (shape(4, *block),) * 2,
        (traveltime, residual, slowness, attenuation),
        vmem=60 << 20,
        in_specs=[hbm] * 4,
        scratch_shapes=[pltpu.SemaphoreType.DMA((8,))],
    )
    got = lax.ppermute(away, "sweep", swap)
    packed = shape(4 * ROWS + columns, crosses)
    centre, to_right, to_left = call(
        pack_kernel, (shape(4, DEEP, columns, crosses), packed, packed), (topography, near, got)
    )
    from_west = lax.ppermute(to_right, "lat", [(i, i + 1) for i in range(lats - 1)])
    from_east = lax.ppermute(to_left, "lat", [(i + 1, i) for i in range(lats - 1)])
    coefs = call(
        coef_kernel,
        (shape(DEEP, 3 * columns, crosses),) * 6,
        (centre, from_west, from_east, topography),
        vmem=16 << 20,
    )

    def hop(value, turn, side):
        pairs = []
        for i in (2 * turn, 2 * turn + 1):
            for k in range(lats):
                if 0 <= k + side < lats:
                    pairs.append((i * lats + k, (i + 2) * lats + k + side))
        return lax.ppermute(value, AXES, pairs)

    near_end = ()
    for turn in range(stages):
        ins = (*coefs, *near_end)
        keep, give, end = call(
            functools.partial(sweep_kernel, turn),
            (shape(*block), shape(*block), shape(columns, crosses)),
            ins,
            in_specs=whole(len(ins) - (2 if turn else 0)) + [hbm] * (2 if turn else 0),
            out_specs=[hbm, hbm] + whole(1),
            input_output_aliases={9: 0, 10: 1} if turn else {},
            scratch_shapes=[VM((DEEP, columns, crosses), F32), pltpu.SemaphoreType.DMA((2,))],
        )
        if turn < stages - 1:
            low, high, own = hop(end, turn, 1), hop(end, turn, -1), hop(end, turn, 0)
            near_end = (low, own, high, keep, give)
    given = lax.ppermute(give, "sweep", swap)
    return call(finish_kernel, (shape(2, *block), shape(*block)), (keep, given, slowness))


def solution(mesh):
    in_specs = (
        P(None, "sweep", "lat", None),
        P(None, "sweep", "lat", None),
        P("sweep", "lat", None),
        P("sweep", "lat", None),
        P("lat", None),
    )
    out_specs = (P(None, "sweep", "lat", None), P("sweep", "lat", None))
    return jax.shard_map(shards, mesh=mesh, in_specs=in_specs, out_specs=out_specs, check_vma=False)
```

```python
import functools
import jax
import jax.numpy as jnp
from jax import lax
from jax.experimental import pallas as pl
from jax.experimental.pallas import tpu as pltpu
from jax.sharding import PartitionSpec as P

F32 = jnp.float32
VM = pltpu.VMEM
HALF = 8
DEEP = 16
COLS = 16
SIDE = 8
EDGE = 5 * SIDE
SKIRT = HALF * SIDE
AXES = ("sweep", "lat")


def whole(count):
    return [pl.BlockSpec(memory_space=VM)] * count


def place():
    s = lax.axis_index("sweep")
    return s // 2, s % 2


def split_kernel(tau, res, slow, att, near_ref, away_ref, sems):
    _, core = place()
    copies = []
    for k, (out, side) in enumerate(((away_ref, 1 - core), (near_ref, core))):
        for a, src in enumerate((tau.at[side], res.at[side], slow, att)):
            copies.append(pltpu.make_async_copy(src, out.at[a], sems.at[4 * k + a]))
    for copy in copies:
        copy.start()
    for copy in copies:
        copy.wait()


def land_kernel(near_hbm, near_ref, sem):
    copy = pltpu.make_async_copy(near_hbm, near_ref, sem)
    copy.start()
    copy.wait()


def pack_edges(mid_ref, base, right_ref, left_ref, row):
    for a in range(4):
        for i in range(5):
            at = a * EDGE + SIDE * i
            right, left = mid_ref[a, base + i, SIDE:COLS], mid_ref[a, base + i, :SIDE]
            if 0 < i < 4:
                far = HALF - i
                right = jnp.where(row >= i, right, pltpu.roll(mid_ref[a, base + far, SIDE:COLS], i, 0))
                left = jnp.where(row < far, left, pltpu.roll(mid_ref[a, base + far, :SIDE], far, 0))
            right_ref[at : at + SIDE] = right
            left_ref[at : at + SIDE] = left


def pack_kernel(topo_ref, near_ref, got_ref, mid_ref, a_right, a_left, b_right, b_left):
    _, core = place()
    mid_ref[:, pl.ds(core * HALF, HALF)] = near_ref[...]
    mid_ref[:, pl.ds((1 - core) * HALF, HALF)] = got_ref[...]
    row = lax.broadcasted_iota(jnp.int32, (SIDE, topo_ref.shape[1]), 0)
    pack_edges(mid_ref, 0, a_right, a_left, row)
    pack_edges(mid_ref, HALF, b_right, b_left, row)
    topo = topo_ref[...].astype(F32)
    for right, left in ((a_right, a_left), (b_right, b_left)):
        right[4 * EDGE :] = topo[SIDE:]
        left[4 * EDGE :] = topo[:SIDE]


def skirt_kernel(mid_ref, topo_ref, right_ref, left_ref):
    row = lax.broadcasted_iota(jnp.int32, (SIDE, topo_ref.shape[1]), 0)
    for a in range(4):
        for i in range(HALF):
            at = a * SKIRT + SIDE * i
            low, high = mid_ref[a, i, :SIDE], mid_ref[a, i, SIDE:COLS]
            right_ref[at : at + SIDE] = jnp.where(row >= i, low, high)
            left_ref[at : at + SIDE] = jnp.where(row < HALF - i, high, low)
    topo = topo_ref[...].astype(F32)
    right_ref[4 * SKIRT :] = topo[:SIDE]
    left_ref[4 * SKIRT :] = topo[SIDE:]


def edge_tiles(west_ref, east_ref, a, i):
    if i <= 4:
        at = a * EDGE + SIDE * i
        return west_ref[at : at + SIDE], east_ref[at : at + SIDE]
    k = HALF - i
    at = a * EDGE + SIDE * k
    return pltpu.roll(west_ref[at : at + SIDE], SIDE - k, 0), pltpu.roll(east_ref[at : at + SIDE], k, 0)


def coef_kernel(base, mid_ref, topo_ref, west_ref, east_ref, *refs):
    outs, skirts = refs[-6:], refs[:-6]
    src_o, mid_o, west_o, east_o, north_o, south_o = outs
    count, rows = src_o.shape[1:]
    halo = (count - COLS) // 2
    stage, _ = place()
    lat, lats = lax.axis_index("lat"), lax.axis_size("lat")
    depth = stage * DEEP + base
    col = lax.broadcasted_iota(jnp.int32, (count, rows), 0)
    cross = lax.broadcasted_iota(jnp.int32, (count, rows), 1)
    row = lax.broadcasted_iota(jnp.int32, (SIDE, rows), 0)
    first, last = cross == 0, cross == rows - 1
    inside = ((col >= halo) | (lat > 0)) & ((col < halo + COLS) | (lat < lats - 1))
    topo = [west_ref[4 * EDGE :], topo_ref[...].astype(F32), east_ref[4 * EDGE :]]
    if skirts:
        topo = [skirts[0][4 * SKIRT :]] + topo + [skirts[1][4 * SKIRT :]]
    topo = jnp.where(inside, jnp.concatenate(topo, axis=0), 1e6)

    def window(a, i):
        west, east = edge_tiles(west_ref, east_ref, a, i)
        tiles = [west, mid_ref[a, base + i], east]
        if skirts:
            at = a * SKIRT + SIDE * i
            far_west, far_east = skirts[0][at : at + SIDE], skirts[1][at : at + SIDE]
            tiles[0] = jnp.where(row >= i, west, far_west)
            tiles[2] = jnp.where(row < HALF - i, east, far_east)
            tiles = [far_west] + tiles + [far_east]
        return jnp.concatenate(tiles, axis=0)

    for i in range(HALF):
        tau = window(0, i)
        slow = window(2, i)
        active = (topo <= (depth + i).astype(F32)).astype(F32)
        step_x = tau - pltpu.roll(tau, 1, 0)
        step_y = tau - jnp.where(first, 0.0, pltpu.roll(tau, 1, 1))
        flat_x = jnp.log(1.0 + jnp.exp(-jnp.abs(step_x)))
        flat_y = jnp.log(1.0 + jnp.exp(-jnp.abs(step_y)))
        edge = tau[:, rows - 128 :]
        edge = jnp.maximum(edge, 0.0) + jnp.log(1.0 + jnp.exp(-jnp.abs(edge)))
        west = jnp.maximum(step_x, 0.0) + flat_x
        east = pltpu.roll(jnp.maximum(-step_x, 0.0) + flat_x, count - 1, 0)
        north = jnp.maximum(step_y, 0.0) + flat_y
        south = pltpu.roll(jnp.maximum(-step_y, 0.0) + flat_y, rows - 1, 1)
        edge = jnp.where(last[:, rows - 128 :], edge, south[:, rows - 128 :])
        south = jnp.concatenate([south[:, : rows - 128], edge], axis=1)
        scale = active / (slow + west + east + north + south + window(3, i))
        src_o[i] = scale * window(1, i)
        mid_o[i] = scale * slow
        west_o[i] = scale * west
        east_o[i] = scale * east
        north_o[i] = jnp.where(first, 0.0, scale * north)
        south_o[i] = jnp.where(last, 0.0, scale * south)


def trim(level, cut):
    return level[cut : level.shape[0] - cut] if cut else level


def march(level, coefs, keep):
    src, mid, west, east, north, south = coefs
    count, rows = src.shape[1:]
    halo = (count - COLS) // 2
    for i in range(HALF):
        need = HALF - 1 - i + keep
        cut = max(halo - (need + SIDE - 1) // SIDE * SIDE, 0)
        span = slice(cut, count - cut)
        if level is None:
            level = src[i, span]
        else:
            wide = level.shape[0]
            down, up = pltpu.roll(level, 1, 0), pltpu.roll(level, wide - 1, 0)
            before, after = pltpu.roll(level, 1, 1), pltpu.roll(level, rows - 1, 1)
            lose = (wide - (count - 2 * cut)) // 2
            level, down, up, before, after = (trim(v, lose) for v in (level, down, up, before, after))
            level = (
                src[i, span]
                + mid[i, span] * level
                + west[i, span] * down
                + east[i, span] * up
                + north[i, span] * before
                + south[i, span] * after
            )
        yield level


def sweep_kernel(turn, half, nlevels, *refs):
    count = 12 if half is None else 6
    coefs = refs[:count]
    levels = refs[count : count + nlevels]
    buf_ref, sems = refs[-2:]
    outs = refs[:-2]
    end_ref = None
    if turn is not None:
        end_ref, outs = outs[-1], outs[:-1]
    keep_ref, give_ref = outs[-2:]
    stage, core = place()
    here = 0 if half is not None else (turn if turn is not None else lax.axis_size("sweep") // 2 - 1)

    def send(part, slot, wait):
        @pl.when(core == part)
        def _():
            copy = pltpu.make_async_copy(buf_ref.at[slot], keep_ref, sems.at[slot])
            copy.wait() if wait else copy.start()

        @pl.when(core != part)
        def _():
            copy = pltpu.make_async_copy(buf_ref.at[slot], give_ref, sems.at[slot])
            copy.wait() if wait else copy.start()

    @pl.when(stage == here)
    def _():
        level = None
        if levels:
            low, own, high = (r[...] for r in levels)
            if half is not None:
                low, high = low[SIDE:], high[:SIDE]
            level = jnp.concatenate([low, own, high], axis=0)
        parts = [(half, coefs, 0)] if half is not None else [(0, coefs[:6], HALF), (1, coefs[6:], 0)]
        for slot, (part, own_coefs, keep) in enumerate(parts):
            for i, plane in enumerate(march(level, own_coefs, keep)):
                level = plane
                margin = (level.shape[0] - COLS) // 2
                buf_ref[slot, i] = level[margin : margin + COLS]
            send(part, slot, False)
        if end_ref is not None:
            margin = (level.shape[0] - COLS) // 2
            end_ref[...] = level[margin : margin + COLS]
        for slot, (part, _, _) in enumerate(parts):
            send(part, slot, True)


def finish_kernel(kept_ref, got_ref, slow_ref, adjoint_ref, gradient_ref):
    _, core = place()
    own, got = kept_ref[...], got_ref[...]
    adjoint_ref[core] = own
    adjoint_ref[1 - core] = got
    gradient_ref[...] = slow_ref[...] * (own + got)


def shards(traveltime, residual, slowness, attenuation, topography):
    columns, crosses = topography.shape
    sweeps, lats = lax.axis_size("sweep"), lax.axis_size("lat")
    stages = sweeps // 2
    hbm = pl.BlockSpec(memory_space=pltpu.HBM)
    block = (HALF, columns, crosses)

    def shape(*dims):
        return jax.ShapeDtypeStruct(dims, F32)

    def call(kernel, outs, ins, vmem=4 << 20, in_specs=None, out_specs=None, **kw):
        return pl.pallas_call(
            kernel,
            out_shape=outs,
            in_specs=in_specs or whole(len(ins)),
            out_specs=out_specs or whole(len(outs)),
            compiler_params=pltpu.CompilerParams(vmem_limit_bytes=vmem),
            **kw,
        )(*ins)

    swap = [(i, i ^ 1) for i in range(sweeps)]
    near, away = call(
        split_kernel,
        (shape(4, *block),) * 2,
        (traveltime, residual, slowness, attenuation),
        vmem=60 << 20,
        in_specs=[hbm] * 4,
        scratch_shapes=[pltpu.SemaphoreType.DMA((8,))],
    )
    got = lax.ppermute(away, "sweep", swap)
    (landed,) = call(
        land_kernel,
        (shape(4, *block),),
        (near,),
        in_specs=[hbm],
        scratch_shapes=[pltpu.SemaphoreType.DMA],
        cost_estimate=pl.CostEstimate(flops=0, bytes_accessed=2 << 20, transcendentals=0),
    )
    edges = shape(4 * EDGE + SIDE, crosses)
    mid, *packs = call(pack_kernel, (shape(4, DEEP, columns, crosses),) + (edges,) * 4, (topography, landed, got))
    rightward = [(i, i + 1) for i in range(lats - 1)]
    leftward = [(i + 1, i) for i in range(lats - 1)]
    a_west = lax.ppermute(packs[0], "lat", rightward)
    a_east = lax.ppermute(packs[1], "lat", leftward)
    b_west = lax.ppermute(packs[2], "lat", rightward)
    b_east = lax.ppermute(packs[3], "lat", leftward)

    skirt = shape(4 * SKIRT + SIDE, crosses)
    to_right, to_left = call(skirt_kernel, (skirt,) * 2, (mid, topography))
    upper = [i * lats for i in range(2, sweeps)]
    c_west = lax.ppermute(to_right, AXES, [(i + a, i + b) for i in upper for a, b in rightward])
    c_east = lax.ppermute(to_left, AXES, [(i + a, i + b) for i in upper for a, b in leftward])

    def coef(base, width, ins):
        return call(
            functools.partial(coef_kernel, base),
            (shape(HALF, columns + 2 * width, crosses),) * 6,
            (mid, topography, *ins),
            vmem=8 << 20,
            cost_estimate=pl.CostEstimate(flops=10 << 20, bytes_accessed=3 << 20, transcendentals=0),
        )

    def hop(value, turn, ahead, side):
        pairs = []
        for i in (2 * turn, 2 * turn + 1):
            for k in range(lats):
                if 0 <= k + side < lats:
                    pairs.append((i * lats + k, (i + 2 * ahead) * lats + k + side))
        return lax.ppermute(value, AXES, pairs)

    def sweep(turn, half, coefs, levels, fields):
        ins = (*coefs, *levels, *fields)
        ends = () if turn is None else (shape(columns, crosses),)
        slots = 2 if half is None else 1
        at = len(ins) - 2
        keep, give, *end = call(
            functools.partial(sweep_kernel, turn, half, len(levels)),
            (shape(*block), shape(*block)) + ends,
            ins,
            in_specs=whole(len(coefs) + len(levels)) + [hbm] * len(fields),
            out_specs=[hbm, hbm] + whole(len(ends)),
            input_output_aliases={at: 0, at + 1: 1} if fields else {},
            scratch_shapes=[VM((slots, *block), F32), pltpu.SemaphoreType.DMA((2,))],
        )
        return (keep, give), end

    coef_a = coef(0, SIDE, (a_west, a_east))
    fields, (end,) = sweep(0, 0, coef_a, (), ())
    low, high = hop(end, 0, 0, 1), hop(end, 0, 0, -1)
    coef_b = coef(HALF, SIDE, (b_west, b_east))
    fields, (end,) = sweep(0, 1, coef_b, (low, end, high), fields)

    def forward(end, turn):
        low = hop(end, turn, 1, 1)
        high = hop(end, turn, 1, -1)
        own = hop(end, turn, 1, 0)
        return low, own, high

    levels = forward(end, 0)
    coef_c = coef(0, COLS, (a_west, a_east, c_west, c_east))
    for turn in range(1, stages):
        more = turn < stages - 1
        fields, end = sweep(turn if more else None, None, (*coef_c, *coef_b), levels, fields)
        if more:
            levels = forward(end[0], turn)
    keep, give = fields
    given = lax.ppermute(give, "sweep", swap)
    return call(finish_kernel, (shape(2, *block), shape(*block)), (keep, given, slowness))


def solution(mesh):
    in_specs = (
        P(None, "sweep", "lat", None),
        P(None, "sweep", "lat", None),
        P("sweep", "lat", None),
        P("sweep", "lat", None),
        P("lat", None),
    )
    out_specs = (P(None, "sweep", "lat", None), P("sweep", "lat", None))
    return jax.shard_map(shards, mesh=mesh, in_specs=in_specs, out_specs=out_specs, check_vma=False)
```
